32 devices in a mesh: dp: 16 (over z, y, x), tensor: 2 (over core).
Axes of the slice: x: 2, y: 2, z: 4, core: 2. Of those that a mesh axis runs over, the one named last changes fastest.
Arguments:
- layer_in: bfloat16 [8192, 768], P(('dp', 'tensor')), may hold values from -6 to 6
- norm1_gain: bfloat16 [768], P('tensor'), may hold values from 0.5 to 1.5
- qkv_weight: bfloat16 [768, 2304], P('tensor'), may hold values from -0.21875 to 0.21875
- out_weight: bfloat16 [768, 768], P('tensor'), may hold values from -4 to 4
- norm2_gain: bfloat16 [768], P('tensor'), may hold values from 0.5 to 1.5
- mlp_weight: bfloat16 [3, 768, 1152], P(None, None, 'tensor'), may hold values from -0.21875 to 0.21875
- cotangent: bfloat16 [8192, 768], P(('dp', 'tensor')), may hold values from -6 to 6
Outputs:
- layer_out: bfloat16 [8192, 768], P(('dp', 'tensor'))
- input_grad: float32 [8192, 768], P(('dp', 'tensor'))
- norm1_grad: float32 [768], P('tensor')
- qkv_grad: float32 [768, 2304], P('tensor')
- out_grad: float32 [768, 768], P('tensor')
- norm2_grad: float32 [768], P('tensor')
- mlp_grad: float32 [3, 768, 1152], P(None, None, 'tensor')
The draws below stay inside these ranges and needn't reach their ends.
All inputs are finite; a program needn't handle non-finite values.
Results may differ from the reference program's by a relative error of at most 0.023.
Values may be sent and summed in bfloat16 or wider, within the bound.
A program may use at most 128 MiB of HBM per device.

```python
import jax
import jax.numpy as jnp
from jax import lax

D = 768
HEADS = 12
HEAD_DIM = 64
FF = 1152
SEQ = 512
TOKENS = 8192


def shard_levels(stream_key, dims, pieces, low, top_value):
    loudness, own = 1.0, jax.random.fold_in(stream_key, 6)
    for dim, blocks in pieces:
        heights = jnp.exp(jax.random.uniform(jax.random.fold_in(own, dim), (blocks,), jnp.float32, low / len(pieces), top_value / len(pieces)))
        loudness = loudness * jnp.repeat(heights, dims[dim] // blocks).reshape([-1 if axis == dim else 1 for axis in range(len(dims))])
    return loudness


def noise(rng, shape, deviation, reach, shards=(), kind=jnp.bfloat16):
    loudness = shard_levels(rng, shape, shards, -0.22, 0.18) if shards else 1.0
    drawn = jax.random.normal(rng, shape, jnp.float32) * deviation * loudness
    return jnp.minimum(jnp.maximum(drawn, -reach), reach).astype(kind)


def setup_inputs(seed: int = 0) -> dict:
    key_of = jax.random.split(jax.random.key(seed), 8)
    layer_in = noise(key_of[0], (TOKENS, D), 1.0, 6.0, ((0, 32),))
    norm1_gain = jnp.clip(1.0 + 0.1 * jax.random.normal(key_of[1], (D,), jnp.float32), 0.5, 1.5).astype(jnp.bfloat16)
    qkv_weight = noise(key_of[2], (D, 3 * D), D ** -0.5, 0.21875, ((0, 2),))
    out_weight = noise(key_of[3], (D, D), (max(D // 384, 1)) ** -0.5, 4.0, ((0, 2),))
    norm2_gain = jnp.clip(1.0 + 0.1 * jax.random.normal(key_of[4], (D,), jnp.float32), 0.5, 1.5).astype(jnp.bfloat16)
    mlp_weight = noise(key_of[5], (3, D, FF), D ** -0.5, 0.21875, ((2, 2),))
    cotangent = noise(key_of[6], (TOKENS, D), 1.0, 6.0, ((0, 32),))
    return dict(layer_in=layer_in, norm1_gain=norm1_gain, qkv_weight=qkv_weight, out_weight=out_weight, norm2_gain=norm2_gain, mlp_weight=mlp_weight, cotangent=cotangent)


EPS = 1e-05
THETA = 160000.0

def rope_tables(positions):
    half = HEAD_DIM // 2
    freq = THETA ** (-jnp.arange(half).astype(jnp.float32) * 2.0 / HEAD_DIM)
    angle = positions.astype(jnp.float32)[:, None] * freq[None, :]
    return (jnp.cos(angle)[:, None, :], jnp.sin(angle)[:, None, :])

def rotate(values, cosine, sine):
    half = HEAD_DIM // 2
    first, second = (values[..., :half], values[..., half:])
    return jnp.concatenate([first * cosine - second * sine, second * cosine + first * sine], -1)

def unrotate(values, cosine, sine):
    half = HEAD_DIM // 2
    first, second = (values[..., :half], values[..., half:])
    return jnp.concatenate([first * cosine + second * sine, second * cosine - first * sine], -1)

def layer_norm_forward(values, gain):
    centred = values - lax.optimization_barrier(jnp.mean(values, -1, keepdims=True))
    inverse = lax.rsqrt(lax.optimization_barrier(jnp.mean(centred * centred, -1, keepdims=True)) + EPS)
    normed = centred * inverse
    return (normed * gain, normed, inverse)

def layer_norm_backward(upstream, normed, inverse, gain):
    scaled = upstream * gain
    back = inverse * (scaled - lax.optimization_barrier(jnp.mean(scaled, -1, keepdims=True)) - normed * lax.optimization_barrier(jnp.mean(scaled * normed, -1, keepdims=True)))
    return (back, lax.optimization_barrier(jnp.sum(upstream * normed, 0)))

def gelu_parts(values):
    cdf = 0.5 * (1.0 + jax.scipy.special.erf(values * 0.7071067811865476))
    density = jnp.exp(-0.5 * values * values) * 0.3989422804014327
    return (values * cdf, cdf + values * density)

def reference(layer_in, norm1_gain, qkv_weight, out_weight, norm2_gain, mlp_weight, cotangent):
    f32 = jnp.float32
    bf16 = jnp.bfloat16
    count = TOKENS // SEQ
    first_norm_gain = norm1_gain.astype(f32)
    second_norm_gain = norm2_gain.astype(f32)
    scale = HEAD_DIM ** (-0.5)
    cosine, sine = rope_tables(jnp.arange(SEQ).astype(jnp.int32))

    def one_sequence(carry, inputs):
        layer_seq, cot_seq = inputs
        input_float_rows = layer_seq.astype(f32)
        first_normed_rows, standardized_first, inverse_deviation_first = layer_norm_forward(input_float_rows, first_norm_gain)
        h1 = first_normed_rows.astype(bf16)
        qkv = jnp.dot(h1, qkv_weight, preferred_element_type=f32).reshape(SEQ, 3, HEADS, HEAD_DIM)
        query = rotate(qkv[:, 0], cosine, sine).astype(bf16)
        keys = rotate(qkv[:, 1], cosine, sine).astype(bf16)
        values = qkv[:, 2].astype(bf16)
        qf, kf, vf = (query.astype(f32), keys.astype(f32), values.astype(f32))
        scores = jnp.einsum('qhd,khd->hqk', qf, kf) * scale
        total = jnp.log(lax.optimization_barrier(jnp.sum(jnp.exp(scores), -1)))
        probs = jnp.exp(scores - total[..., None])
        probs_b = probs.astype(bf16)
        attended = jnp.einsum('hqk,khd->qhd', probs_b.astype(f32), vf).astype(bf16).reshape(SEQ, D)
        attention_mixed = input_float_rows + jnp.dot(attended, out_weight, preferred_element_type=f32)
        second_normed_rows, standardized_second, inverse_deviation_second = layer_norm_forward(attention_mixed, second_norm_gain)
        h2 = second_normed_rows.astype(bf16)
        gate_pre = jnp.dot(h2, mlp_weight[0], preferred_element_type=f32)
        up_pre = jnp.dot(h2, mlp_weight[1], preferred_element_type=f32)
        gel, slope = gelu_parts(gate_pre)
        hidden = (gel * up_pre).astype(bf16)
        out_f = attention_mixed + jnp.dot(hidden, mlp_weight[2].T, preferred_element_type=f32)
        layer_out = out_f.astype(bf16)
        dz_f = cot_seq.astype(f32)
        grad_hidden = jnp.dot(cot_seq, mlp_weight[2], preferred_element_type=f32)
        grad_gate = (grad_hidden * up_pre * slope).astype(bf16)
        grad_up = (grad_hidden * gel).astype(bf16)
        grad_mlp = jnp.stack([jnp.dot(h2.T, grad_gate, preferred_element_type=f32), jnp.dot(h2.T, grad_up, preferred_element_type=f32), jnp.dot(cot_seq.T, hidden, preferred_element_type=f32)])
        gradient_hidden_second = jnp.dot(grad_gate, mlp_weight[0].T, preferred_element_type=f32) + jnp.dot(grad_up, mlp_weight[1].T, preferred_element_type=f32)
        second_norm_backward, gradient_gain_second = layer_norm_backward(gradient_hidden_second, standardized_second, inverse_deviation_second, second_norm_gain)
        grad_mixed = dz_f + second_norm_backward
        grad_mixed_b = grad_mixed.astype(bf16)
        grad_wout = jnp.dot(attended.T, grad_mixed_b, preferred_element_type=f32)
        grad_att = jnp.dot(grad_mixed_b, out_weight.T, preferred_element_type=f32).astype(bf16).reshape(SEQ, HEADS, HEAD_DIM)
        gaf = grad_att.astype(f32)
        grad_probs = jnp.einsum('qhd,khd->hqk', gaf, vf)
        delta = jnp.einsum('qhd,qhd->hq', gaf, attended.reshape(SEQ, HEADS, HEAD_DIM).astype(f32))
        grad_scores = (probs * (grad_probs - delta[..., None])).astype(bf16).astype(f32)
        grad_query = jnp.einsum('hqk,khd->qhd', grad_scores, kf) * scale
        grad_keys = jnp.einsum('hqk,qhd->khd', grad_scores, qf) * scale
        grad_values = jnp.einsum('hqk,qhd->khd', probs_b.astype(f32), gaf)
        grad_q = unrotate(grad_query, cosine, sine).reshape(SEQ, D)
        grad_k = unrotate(grad_keys, cosine, sine).reshape(SEQ, D)
        grad_qkv = jnp.concatenate([grad_q, grad_k, grad_values.reshape(SEQ, D)], 1).astype(bf16)
        grad_wqkv = jnp.dot(h1.T, grad_qkv, preferred_element_type=f32)
        gradient_hidden_first = jnp.dot(grad_qkv, qkv_weight.T, preferred_element_type=f32)
        first_norm_backward, gradient_gain_first = layer_norm_backward(gradient_hidden_first, standardized_first, inverse_deviation_first, first_norm_gain)
        input_grad = grad_mixed + first_norm_backward
        acc_qkv, acc_out, acc_g1, acc_g2, acc_mlp = carry
        carry = (acc_qkv + grad_wqkv, acc_out + grad_wout, acc_g1 + gradient_gain_first, acc_g2 + gradient_gain_second, acc_mlp + grad_mlp)
        return (carry, (layer_out, input_grad))
    start = (jnp.zeros((D, 3 * D), f32), jnp.zeros((D, D), f32), jnp.zeros((D,), f32), jnp.zeros((D,), f32), jnp.zeros((3, D, FF), f32))
    carry, outputs = lax.scan(one_sequence, start, (layer_in.reshape(count, SEQ, D), cotangent.reshape(count, SEQ, D)))
    layer_out = outputs[0].reshape(TOKENS, D)
    input_grad = outputs[1].reshape(TOKENS, D)
    return (layer_out, input_grad, carry[2], carry[0], carry[1], carry[3], carry[4])
```

```python
import jax
import jax.numpy as jnp
from jax import lax
from jax.experimental import pallas as pl
from jax.experimental.pallas import tpu as pltpu
from jax.sharding import PartitionSpec as P

HEADS = 12
HEAD_DIM = 64
SEQ = 512


EPS = 1e-05
THETA = 160000.0


def swapped(value, axis, distance):
    mask = 2**distance
    pairs = [(source, source ^ mask) for source in range(lax.axis_size(axis))]
    return lax.ppermute(value, axis, pairs)


def rope_tables(positions):
    half = HEAD_DIM // 2
    freq = THETA ** (-jnp.arange(half).astype(jnp.float32) * 2.0 / HEAD_DIM)
    angle = positions.astype(jnp.float32)[:, None] * freq[None, :]
    return (jnp.cos(angle)[:, None, :], jnp.sin(angle)[:, None, :])


def rotate(values, cosine, sine):
    half = HEAD_DIM // 2
    first, second = (values[..., :half], values[..., half:])
    return jnp.concatenate([first * cosine - second * sine, second * cosine + first * sine], -1)


def unrotate(values, cosine, sine):
    half = HEAD_DIM // 2
    first, second = (values[..., :half], values[..., half:])
    return jnp.concatenate([first * cosine + second * sine, second * cosine - first * sine], -1)


def layer_norm_forward(values, gain):
    centred = values - jnp.mean(values, -1, keepdims=True)
    inverse = lax.rsqrt(jnp.mean(centred * centred, -1, keepdims=True) + EPS)
    normed = centred * inverse
    return (normed * gain, normed, inverse)


def layer_norm_backward(upstream, normed, inverse, gain):
    scaled = upstream * gain
    back = inverse * (
        scaled
        - jnp.mean(scaled, -1, keepdims=True)
        - normed * jnp.mean(scaled * normed, -1, keepdims=True)
    )
    return (back, jnp.sum(upstream * normed, 0))


def gelu_parts(values):
    cdf = 0.5 * (1.0 + jax.scipy.special.erf(values * 0.7071067811865476))
    density = jnp.exp(-0.5 * values * values) * 0.3989422804014327
    return (values * cdf, cdf + values * density)


def right_product(left, weight):
    return lax.dot_general(
        left, weight, (((1,), (1,)), ((), ())), preferred_element_type=jnp.float32
    )


def left_product(left, right):
    return lax.dot_general(
        left, right, (((0,), (0,)), ((), ())), preferred_element_type=jnp.float32
    )


def collect_keys(key_own, value_own, position_slot):
    pair = (key_own, value_own)
    far_key, far_value = swapped((pair[0], pair[1]), "tensor", 0)
    upper = (position_slot >> 0) % 2 == 1
    pair = (
        jnp.where(
            upper, jnp.concatenate([far_key, pair[0]], 0), jnp.concatenate([pair[0], far_key], 0)
        ),
        jnp.where(
            upper,
            jnp.concatenate([far_value, pair[1]], 0),
            jnp.concatenate([pair[1], far_value], 0),
        ),
    )
    return pair


def return_grads(key_grad, value_grad, position_slot):
    pair = (key_grad, value_grad)
    middle = pair[0].shape[0] // 2
    upper = (position_slot >> 0) % 2 == 1
    keep_key = jnp.where(upper, pair[0][middle:], pair[0][:middle])
    send_key = jnp.where(upper, pair[0][:middle], pair[0][middle:])
    keep_value = jnp.where(upper, pair[1][middle:], pair[1][:middle])
    send_value = jnp.where(upper, pair[1][:middle], pair[1][middle:])
    back_key = swapped(send_key.astype(jnp.bfloat16), "tensor", 0).astype(send_key.dtype)
    back_value = swapped(send_value.astype(jnp.bfloat16), "tensor", 0).astype(send_value.dtype)
    pair = (keep_key + back_key, keep_value + back_value)
    return pair


def bit_count(size):
    return size.bit_length() - 1


def gather_rows(value, axis):
    index = lax.axis_index(axis)
    for distance in range(bit_count(lax.axis_size(axis))):
        other = swapped(value, axis, distance)
        upper = (index >> distance) % 2 == 1
        value = jnp.where(
            upper, jnp.concatenate([other, value], 0), jnp.concatenate([value, other], 0)
        )
    return value


def scatter_sum(value, axis, wire):
    index = lax.axis_index(axis)
    for distance in reversed(range(bit_count(lax.axis_size(axis)))):
        middle = value.shape[0] // 2
        upper = (index >> distance) % 2 == 1
        keep = jnp.where(upper, value[middle:], value[:middle])
        send = jnp.where(upper, value[:middle], value[middle:])
        value = keep + swapped(send.astype(wire), axis, distance).astype(value.dtype)
    return value


TILE = (16, 128)
STREAMS = 3
MESH = pl.DeviceIdType.MESH


def to_tiles(value):
    rows, columns = value.shape
    value = value.reshape(rows // TILE[0], TILE[0], columns // TILE[1], TILE[1])
    return value.transpose(0, 2, 1, 3).reshape(-1, *TILE)


def from_tiles(value, rows, columns):
    value = value.reshape(rows // TILE[0], columns // TILE[1], *TILE)
    return value.transpose(0, 2, 1, 3).reshape(rows, columns)


def add_into(result, target, start, source, source_start, count):
    step = 8
    while count % step:
        step //= 2

    def one(index, carry):
        place = pl.ds(start + index * step, step)
        result[place] = target[place] + source[pl.ds(source_start + index * step, step)]
        return carry

    lax.fori_loop(0, count // step, one, 0)


def bit_of(index, bit):
    return lax.rem(lax.div(index, 2**bit), 2)


def partner_of(index, bit):
    return index + (1 - 2 * bit_of(index, bit)) * 2**bit


def reduce_kernel(
    dp_bits, tensor_bits, shared_ref, local_ref, out_ref, acc, work, got_tensor, got, full, sems
):
    send_sem, recv_sem, tensor_send, tensor_recv, load_sem = sems
    me = lax.axis_index("dp")
    slot = lax.axis_index("tensor")
    shared = shared_ref.shape[0] // 2**tensor_bits
    local = local_ref.shape[0]
    total = shared + local

    barrier = pltpu.get_barrier_semaphore()
    for bit in range(dp_bits):
        pl.semaphore_signal(
            barrier, inc=1, device_id=(partner_of(me, bit), slot), device_id_type=MESH
        )
    for bit in range(tensor_bits):
        pl.semaphore_signal(
            barrier, inc=1, device_id=(me, partner_of(slot, bit)), device_id_type=MESH
        )
    load_local = pltpu.make_async_copy(local_ref, acc.at[pl.ds(shared, local)], load_sem.at[0])
    load_local.start()
    load_shared = pltpu.make_async_copy(shared_ref, work, load_sem.at[1])
    load_shared.start()
    load_shared.wait()
    pl.semaphore_wait(barrier, dp_bits + tensor_bits)

    start, length, place = 0, shared * 2**tensor_bits, 0
    for stage, bit in enumerate(reversed(range(tensor_bits))):
        length //= 2
        mine = bit_of(slot, bit)
        copy = pltpu.make_async_remote_copy(
            src_ref=work.at[pl.ds(start + (1 - mine) * length, length)],
            dst_ref=got_tensor.at[pl.ds(place, length)],
            send_sem=tensor_send.at[stage],
            recv_sem=tensor_recv.at[stage],
            device_id=(me, partner_of(slot, bit)),
            device_id_type=MESH,
        )
        copy.start()
        copy.wait()
        start = start + mine * length
        add_into(work, work, start, got_tensor, place, length)
        place += length

    def move(index, carry):
        acc[index] = work[start + index]
        return carry

    lax.fori_loop(0, shared, move, 0)
    load_local.wait()

    share = total // STREAMS
    lowest = [(0, 1, 2, 3), (1, 2, 3, 0), (2, 3, 0, 1)]
    orders = []
    for stream in range(STREAMS):
        if dp_bits == 4:
            orders.append(lowest[stream])
        else:
            orders.append(tuple((stream + bit) % dp_bits for bit in range(dp_bits)))
    starts = [[stream * share] for stream in range(STREAMS)]
    lengths = [share >> stage for stage in range(dp_bits + 1)]
    arrive = [share - lengths[stage] for stage in range(dp_bits)]

    def reduce_copy(stream, stage):
        bit = orders[stream][stage]
        half = lengths[stage + 1]
        begin = starts[stream][stage]
        return pltpu.make_async_remote_copy(
            src_ref=acc.at[pl.ds(begin + (1 - bit_of(me, bit)) * half, half)],
            dst_ref=got.at[stream, pl.ds(arrive[stage], half)],
            send_sem=send_sem.at[stream, stage],
            recv_sem=recv_sem.at[stream, stage],
            device_id=(partner_of(me, bit), slot),
            device_id_type=MESH,
        )

    def gather_copy(stream, stage):
        bit = orders[stream][stage]
        half = lengths[stage + 1]
        region = pl.ds(starts[stream][stage + 1], half)
        return pltpu.make_async_remote_copy(
            src_ref=full.at[region],
            dst_ref=full.at[region],
            send_sem=send_sem.at[stream, dp_bits + stage],
            recv_sem=recv_sem.at[stream, dp_bits + stage],
            device_id=(partner_of(me, bit), slot),
            device_id_type=MESH,
        )

    flying = []
    for stream in range(STREAMS):
        copy = reduce_copy(stream, 0)
        copy.start()
        flying.append(copy)
    for stage in range(dp_bits):
        for stream in range(STREAMS):
            flying[stream].wait()
            half = lengths[stage + 1]
            begin = starts[stream][stage] + bit_of(me, orders[stream][stage]) * half
            starts[stream].append(begin)
            add_into(acc if stage + 1 < dp_bits else full, acc, begin, got.at[stream], arrive[stage], half)
            if stage + 1 < dp_bits:
                copy = reduce_copy(stream, stage + 1)
            else:
                copy = gather_copy(stream, stage)
            copy.start()
            flying[stream] = copy
    for stage in reversed(range(dp_bits)):
        for stream in range(STREAMS):
            flying[stream].wait()
            if stage:
                copy = gather_copy(stream, stage - 1)
                copy.start()
                flying[stream] = copy
    store = pltpu.make_async_copy(full, out_ref, load_sem.at[0])
    store.start()
    store.wait()


def reduce_gradients(shared_tiles, local_tiles):
    dp_bits = bit_count(lax.axis_size("dp"))
    tensor_bits = bit_count(lax.axis_size("tensor"))
    shared = shared_tiles.shape[0] >> tensor_bits
    local = local_tiles.shape[0]
    total = shared + local
    share = total // STREAMS
    bf16 = jnp.bfloat16
    dma = pltpu.SemaphoreType.DMA

    def kernel(shared_ref, local_ref, out_ref, acc, work, got_tensor, got, full, *sems):
        reduce_kernel(
            dp_bits, tensor_bits, shared_ref, local_ref, out_ref, acc, work, got_tensor, got, full, sems
        )

    return pl.pallas_call(
        kernel,
        out_shape=jax.ShapeDtypeStruct((total, *TILE), bf16),
        in_specs=[pl.BlockSpec(memory_space=pl.ANY)] * 2,
        out_specs=pl.BlockSpec(memory_space=pl.ANY),
        scratch_shapes=[
            pltpu.VMEM((total, *TILE), bf16),
            pltpu.VMEM(shared_tiles.shape, bf16),
            pltpu.VMEM((max(1, shared_tiles.shape[0] - shared), *TILE), bf16),
            pltpu.VMEM((STREAMS, share - (share >> dp_bits), *TILE), bf16),
            pltpu.VMEM((total, *TILE), bf16),
            dma((STREAMS, 2 * dp_bits)),
            dma((STREAMS, 2 * dp_bits)),
            dma((max(1, tensor_bits),)),
            dma((max(1, tensor_bits),)),
            dma((2,)),
        ],
        compiler_params=pltpu.CompilerParams(
            collective_id=0, has_side_effects=True, vmem_limit_bytes=40 * 2**20
        ),
        name="reduce_gradients",
    )(shared_tiles, local_tiles)


def body(layer_in, norm1_gain, qkv_weight, out_weight, norm2_gain, mlp_weight, cotangent):
    f32 = jnp.float32
    bf16 = jnp.bfloat16
    rows = layer_in.shape[0]
    width = layer_in.shape[1]
    span = SEQ // rows
    scale = HEAD_DIM ** (-0.5)
    first_norm_gain, second_norm_gain, w_qkv, w_out = (
        gather_rows(norm1_gain, "tensor"),
        gather_rows(norm2_gain, "tensor"),
        gather_rows(qkv_weight, "tensor"),
        gather_rows(out_weight, "tensor"),
    )
    first_norm_gain = first_norm_gain.astype(f32)
    second_norm_gain = second_norm_gain.astype(f32)
    position_slot = lax.axis_index("tensor") % span
    cosine, sine = rope_tables(position_slot * rows + jnp.arange(rows, dtype=jnp.int32))
    input_float_rows = layer_in.astype(f32)
    first_normed_rows, standardized_first, inverse_deviation_first = layer_norm_forward(
        input_float_rows, first_norm_gain
    )
    h1 = first_normed_rows.astype(bf16)
    qkv = jnp.dot(h1, w_qkv, preferred_element_type=f32)
    query = rotate(qkv[:, :width].reshape(rows, HEADS, HEAD_DIM), cosine, sine).astype(bf16)
    key_own = (
        rotate(qkv[:, width : 2 * width].reshape(rows, HEADS, HEAD_DIM), cosine, sine)
        .astype(bf16)
        .reshape(rows, width)
    )
    value_own = qkv[:, 2 * width :].astype(bf16)
    key_all, value_all = collect_keys(key_own, value_own, position_slot)
    keys = key_all.reshape(SEQ, HEADS, HEAD_DIM)
    values = value_all.reshape(SEQ, HEADS, HEAD_DIM)
    scores = jnp.einsum("qhd,khd->hqk", query, keys, preferred_element_type=f32) * scale
    total = jnp.log(jnp.sum(jnp.exp(scores), -1))
    probs_b = jnp.exp(scores - total[..., None]).astype(bf16)
    attended = (
        jnp.einsum("hqk,khd->qhd", probs_b, values, preferred_element_type=f32)
        .astype(bf16)
        .reshape(rows, width)
    )
    attention_mixed = input_float_rows + jnp.dot(attended, w_out, preferred_element_type=f32)
    second_normed_rows, standardized_second, inverse_deviation_second = layer_norm_forward(
        attention_mixed, second_norm_gain
    )
    h2 = second_normed_rows.astype(bf16)
    dz_f = cotangent.astype(f32)
    group = lax.all_gather(h2, "tensor", axis=0, tiled=True)
    gate_pre = jnp.dot(group, mlp_weight[0], preferred_element_type=f32)
    up_pre = jnp.dot(group, mlp_weight[1], preferred_element_type=f32)
    gel, slope = gelu_parts(gate_pre)
    hidden = (gel * up_pre).astype(bf16)
    branch = scatter_sum(right_product(hidden, mlp_weight[2]), "tensor", bf16)
    layer_out = (attention_mixed + branch).astype(bf16)
    grad_group = lax.all_gather(cotangent, "tensor", axis=0, tiled=True)
    grad_hidden = jnp.dot(grad_group, mlp_weight[2], preferred_element_type=f32)
    grad_gate = (grad_hidden * up_pre * slope).astype(bf16)
    grad_up = (grad_hidden * gel).astype(bf16)
    local_tiles = [
        to_tiles(left_product(grad_gate, group).astype(bf16)),
        to_tiles(left_product(grad_up, group).astype(bf16)),
        to_tiles(left_product(hidden, grad_group).astype(bf16)),
    ]
    gradient_hidden_second = scatter_sum(
        right_product(grad_gate, mlp_weight[0]) + right_product(grad_up, mlp_weight[1]),
        "tensor",
        bf16,
    )
    second_norm_backward, gradient_gain_second = layer_norm_backward(
        gradient_hidden_second, standardized_second, inverse_deviation_second, second_norm_gain
    )
    grad_mixed = dz_f + second_norm_backward
    grad_mixed_b = grad_mixed.astype(bf16)
    grad_wout = left_product(attended, grad_mixed_b)
    grad_att = right_product(grad_mixed_b, w_out).astype(bf16).reshape(rows, HEADS, HEAD_DIM)
    scores = jnp.einsum("qhd,khd->hqk", query, keys, preferred_element_type=f32) * scale
    probs = jnp.exp(scores - total[..., None])
    probs_b = probs.astype(bf16)
    grad_probs = jnp.einsum("qhd,khd->hqk", grad_att, values, preferred_element_type=f32)
    delta = jnp.einsum(
        "qhd,qhd->hq", grad_att.astype(f32), attended.reshape(rows, HEADS, HEAD_DIM).astype(f32)
    )
    grad_scores = (probs * (grad_probs - delta[..., None])).astype(bf16)
    grad_query = jnp.einsum("hqk,khd->qhd", grad_scores, keys, preferred_element_type=f32) * scale
    grad_keys = jnp.einsum("hqk,qhd->khd", grad_scores, query, preferred_element_type=f32) * scale
    grad_values = jnp.einsum("hqk,qhd->khd", probs_b, grad_att, preferred_element_type=f32)
    key_total, value_total = return_grads(
        grad_keys.reshape(SEQ, width), grad_values.reshape(SEQ, width), position_slot
    )
    grad_q = unrotate(grad_query, cosine, sine).reshape(rows, width)
    grad_k = unrotate(key_total.reshape(rows, HEADS, HEAD_DIM), cosine, sine).reshape(rows, width)
    grad_qkv = jnp.concatenate([grad_q, grad_k, value_total], 1).astype(bf16)
    grad_wqkv = left_product(h1, grad_qkv)
    gradient_hidden_first = right_product(grad_qkv, w_qkv)
    first_norm_backward, gradient_gain_first = layer_norm_backward(
        gradient_hidden_first, standardized_first, inverse_deviation_first, first_norm_gain
    )
    input_grad = grad_mixed + first_norm_backward
    tensor = lax.axis_size("tensor")
    gains = jnp.stack([gradient_gain_first, gradient_gain_second], 1).astype(bf16)
    gains = jnp.pad(gains, ((0, 0), (0, TILE[1] - 2)))
    parts = [
        to_tiles(value.astype(bf16)).reshape(tensor, -1, *TILE)
        for value in (grad_wqkv, grad_wout, gains)
    ]
    local = sum(part.shape[0] for part in local_tiles)
    shared = sum(part.shape[1] for part in parts)
    unit = STREAMS * lax.axis_size("dp")
    filler = -(local + shared) % unit
    if filler:
        local_tiles.append(jnp.zeros((filler, *TILE), bf16))
    summed = reduce_gradients(
        jnp.concatenate(parts, 1).reshape(-1, *TILE), jnp.concatenate(local_tiles, 0)
    )
    own = width // tensor
    sizes = [part.shape[1] for part in parts]
    edges = [0, sizes[0], sizes[0] + sizes[1], shared, shared + local]
    qkv_total, out_total, gain_total, mlp_total = (
        summed[low:high] for low, high in zip(edges[:-1], edges[1:])
    )
    units = mlp_weight.shape[2]
    gain_total = from_tiles(gain_total, own, TILE[1]).astype(f32)
    mlp_total = from_tiles(mlp_total, 3 * units, width).reshape(3, units, width)
    return (
        layer_out,
        input_grad,
        gain_total[:, 0],
        from_tiles(qkv_total, own, 3 * width).astype(f32),
        from_tiles(out_total, own, width).astype(f32),
        gain_total[:, 1],
        mlp_total.transpose(0, 2, 1).astype(f32),
    )


def solution(mesh):
    return jax.shard_map(
        body,
        mesh=mesh,
        in_specs=(
            P(("dp", "tensor"), None),
            P("tensor"),
            P("tensor", None),
            P("tensor", None),
            P("tensor"),
            P(None, None, "tensor"),
            P(("dp", "tensor"), None),
        ),
        out_specs=(
            P(("dp", "tensor"), None),
            P(("dp", "tensor"), None),
            P("tensor"),
            P("tensor", None),
            P("tensor", None),
            P("tensor"),
            P(None, None, "tensor"),
        ),
        check_vma=False,
    )
```

```python
import jax
import jax.numpy as jnp
from jax import lax
from jax.experimental import pallas as pl
from jax.experimental.pallas import tpu as pltpu
from jax.sharding import PartitionSpec as P

HEADS = 12
HEAD_DIM = 64
SEQ = 512


EPS = 1e-05
THETA = 160000.0


def swapped(value, axis, distance):
    mask = 2**distance
    pairs = [(source, source ^ mask) for source in range(lax.axis_size(axis))]
    return lax.ppermute(value, axis, pairs)


def rope_tables(positions):
    half = HEAD_DIM // 2
    freq = THETA ** (-jnp.arange(half).astype(jnp.float32) * 2.0 / HEAD_DIM)
    angle = positions.astype(jnp.float32)[:, None] * freq[None, :]
    return (jnp.cos(angle)[:, None, :], jnp.sin(angle)[:, None, :])


def rotate(values, cosine, sine):
    half = HEAD_DIM // 2
    first, second = (values[..., :half], values[..., half:])
    return jnp.concatenate([first * cosine - second * sine, second * cosine + first * sine], -1)


def unrotate(values, cosine, sine):
    half = HEAD_DIM // 2
    first, second = (values[..., :half], values[..., half:])
    return jnp.concatenate([first * cosine + second * sine, second * cosine - first * sine], -1)


def layer_norm_forward(values, gain):
    centred = values - jnp.mean(values, -1, keepdims=True)
    inverse = lax.rsqrt(jnp.mean(centred * centred, -1, keepdims=True) + EPS)
    normed = centred * inverse
    return (normed * gain, normed, inverse)


def layer_norm_backward(upstream, normed, inverse, gain):
    scaled = upstream * gain
    back = inverse * (
        scaled
        - jnp.mean(scaled, -1, keepdims=True)
        - normed * jnp.mean(scaled * normed, -1, keepdims=True)
    )
    return (back, jnp.sum(upstream * normed, 0))


def gelu_parts(values):
    cdf = 0.5 * (1.0 + jax.scipy.special.erf(values * 0.7071067811865476))
    density = jnp.exp(-0.5 * values * values) * 0.3989422804014327
    return (values * cdf, cdf + values * density)


def right_product(left, weight):
    return lax.dot_general(
        left, weight, (((1,), (1,)), ((), ())), preferred_element_type=jnp.float32
    )


def left_product(left, right):
    return lax.dot_general(
        left, right, (((0,), (0,)), ((), ())), preferred_element_type=jnp.float32
    )


def collect_keys(key_own, value_own, position_slot):
    pair = (key_own, value_own)
    far_key, far_value = swapped((pair[0], pair[1]), "tensor", 0)
    upper = (position_slot >> 0) % 2 == 1
    pair = (
        jnp.where(
            upper, jnp.concatenate([far_key, pair[0]], 0), jnp.concatenate([pair[0], far_key], 0)
        ),
        jnp.where(
            upper,
            jnp.concatenate([far_value, pair[1]], 0),
            jnp.concatenate([pair[1], far_value], 0),
        ),
    )
    return pair


def return_grads(key_grad, value_grad, position_slot):
    pair = (key_grad, value_grad)
    middle = pair[0].shape[0] // 2
    upper = (position_slot >> 0) % 2 == 1
    keep_key = jnp.where(upper, pair[0][middle:], pair[0][:middle])
    send_key = jnp.where(upper, pair[0][:middle], pair[0][middle:])
    keep_value = jnp.where(upper, pair[1][middle:], pair[1][:middle])
    send_value = jnp.where(upper, pair[1][:middle], pair[1][middle:])
    back_key = swapped(send_key.astype(jnp.bfloat16), "tensor", 0).astype(send_key.dtype)
    back_value = swapped(send_value.astype(jnp.bfloat16), "tensor", 0).astype(send_value.dtype)
    pair = (keep_key + back_key, keep_value + back_value)
    return pair


def bit_count(size):
    return size.bit_length() - 1


def gather_rows(value, axis):
    index = lax.axis_index(axis)
    for distance in range(bit_count(lax.axis_size(axis))):
        other = swapped(value, axis, distance)
        upper = (index >> distance) % 2 == 1
        value = jnp.where(
            upper, jnp.concatenate([other, value], 0), jnp.concatenate([value, other], 0)
        )
    return value


def scatter_sum(value, axis, wire):
    index = lax.axis_index(axis)
    for distance in reversed(range(bit_count(lax.axis_size(axis)))):
        middle = value.shape[0] // 2
        upper = (index >> distance) % 2 == 1
        keep = jnp.where(upper, value[middle:], value[:middle])
        send = jnp.where(upper, value[:middle], value[middle:])
        value = keep + swapped(send.astype(wire), axis, distance).astype(value.dtype)
    return value


ROWS = 8
MESH = pl.DeviceIdType.MESH


def to_groups(value):
    return value.reshape(-1, ROWS, value.shape[-1])


def add_into(result, result_start, target, start, source, source_start, count):
    step = 4
    while count % step:
        step //= 2

    def one(index, carry):
        shift = index * step
        result[pl.ds(result_start + shift, step)] = (
            target[pl.ds(start + shift, step)] + source[pl.ds(source_start + shift, step)]
        )
        return carry

    lax.fori_loop(0, count // step, one, 0)


def bit_of(index, bit):
    return lax.rem(lax.div(index, 2**bit), 2)


def partner_of(index, bit):
    return index + (1 - 2 * bit_of(index, bit)) * 2**bit


def stream_plan(total, devices):
    bits = bit_count(devices)
    units = -(-total // devices)
    if bits >= 3:
        rest = tuple(range(2, bits))
        orders = [(0, 1) + rest, rest + (0, 1), (1, 0) + rest]
        weights = [5, 3, 5]
    else:
        orders = [tuple(range(bits))]
        weights = [1]
    orders, weights = orders * 2, weights * 2
    shares = [units * weight // sum(weights) for weight in weights]
    for index in range(units - sum(shares)):
        shares[index % len(shares)] += 1
    plan, begin = [], 0
    for order, share in zip(orders, shares):
        if share:
            plan.append((order, begin, share * devices))
            begin += share * devices
    return plan, begin


def reduce_kernel(
    plan, dp_bits, tensor_bits, groups, units, qkv_ref, out_ref, gain_ref, mlp_ref,
    qkv_to, out_to, gain_to, mlp_to, acc, work, got_tensor, got, full,
    send_sem, recv_sem, tensor_send, tensor_recv, load_sem, mlp_sem,
):
    me = lax.axis_index("dp")
    slot = lax.axis_index("tensor")
    tensor = 2**tensor_bits
    width = acc.shape[-1]
    shared = 4 * groups + 1

    load_mlp = pltpu.make_async_copy(mlp_ref, acc.at[pl.ds(0, units)], mlp_sem.at[0])
    load_mlp.start()
    loads = []
    for part in range(tensor):
        rows = pl.ds(part * groups, groups)
        pairs = [
            (qkv_ref.at[rows, :, pl.ds(block * width, width)], block * groups, groups)
            for block in range(3)
        ]
        pairs.append((out_ref.at[rows], 3 * groups, groups))
        pairs.append((gain_ref.at[pl.ds(part, 1)], 4 * groups, 1))
        for source, place, count in pairs:
            copy = pltpu.make_async_copy(
                source, work.at[pl.ds(part * shared + place, count)], load_sem.at[len(loads)]
            )
            copy.start()
            loads.append(copy)

    barrier = pltpu.get_barrier_semaphore()
    for bit in range(dp_bits):
        pl.semaphore_signal(
            barrier, inc=1, device_id=(partner_of(me, bit), slot), device_id_type=MESH
        )
    for bit in range(tensor_bits):
        pl.semaphore_signal(
            barrier, inc=1, device_id=(me, partner_of(slot, bit)), device_id_type=MESH
        )
    load_mlp.wait()
    pl.semaphore_wait(barrier, dp_bits + tensor_bits)

    starts = [[begin] for _, begin, _ in plan]

    def reduce_copy(stream, stage):
        order, base, share = plan[stream]
        bit = order[stage]
        half = share >> (stage + 1)
        begin = starts[stream][stage]
        return pltpu.make_async_remote_copy(
            src_ref=acc.at[pl.ds(begin + (1 - bit_of(me, bit)) * half, half)],
            dst_ref=got.at[pl.ds(base + share - (share >> stage), half)],
            send_sem=send_sem.at[stream, stage],
            recv_sem=recv_sem.at[stream, stage],
            device_id=(partner_of(me, bit), slot),
            device_id_type=MESH,
        )

    def gather_copy(stream, stage):
        order, _, share = plan[stream]
        region = pl.ds(starts[stream][stage + 1], share >> (stage + 1))
        return pltpu.make_async_remote_copy(
            src_ref=full.at[region],
            dst_ref=full.at[region],
            send_sem=send_sem.at[stream, dp_bits + stage],
            recv_sem=recv_sem.at[stream, dp_bits + stage],
            device_id=(partner_of(me, order[stage]), slot),
            device_id_type=MESH,
        )

    flying = {}
    for stream, (_, base, share) in enumerate(plan):
        if base + share <= units:
            flying[stream] = reduce_copy(stream, 0)
            flying[stream].start()

    for copy in loads:
        copy.wait()
    start, length, place = 0, shared * tensor, 0
    for stage, bit in enumerate(reversed(range(tensor_bits))):
        length //= 2
        mine = bit_of(slot, bit)
        copy = pltpu.make_async_remote_copy(
            src_ref=work.at[pl.ds(start + (1 - mine) * length, length)],
            dst_ref=got_tensor.at[pl.ds(place, length)],
            send_sem=tensor_send.at[stage],
            recv_sem=tensor_recv.at[stage],
            device_id=(me, partner_of(slot, bit)),
            device_id_type=MESH,
        )
        copy.start()
        copy.wait()
        start = start + mine * length
        if stage + 1 < tensor_bits:
            add_into(work, start, work, start, got_tensor, place, length)
        else:
            add_into(acc, units, work, start, got_tensor, place, length)
        place += length
    for stream in range(len(plan)):
        if stream not in flying:
            flying[stream] = reduce_copy(stream, 0)
            flying[stream].start()

    for stage in range(dp_bits):
        for stream, (order, base, share) in enumerate(plan):
            flying[stream].wait()
            half = share >> (stage + 1)
            begin = starts[stream][stage] + bit_of(me, order[stage]) * half
            starts[stream].append(begin)
            last = stage + 1 == dp_bits
            add_into(
                full if last else acc, begin, acc, begin,
                got, base + share - (share >> stage), half,
            )
            copy = gather_copy(stream, stage) if last else reduce_copy(stream, stage + 1)
            copy.start()
            flying[stream] = copy
    for stage in reversed(range(dp_bits)):
        for stream in range(len(plan)):
            flying[stream].wait()
            if stage:
                copy = gather_copy(stream, stage - 1)
                copy.start()
                flying[stream] = copy
    pairs = [(mlp_to, 0, units)]
    for block in range(3):
        target = qkv_to.at[:, :, pl.ds(block * width, width)]
        pairs.append((target, units + block * groups, groups))
    pairs.append((out_to, units + 3 * groups, groups))
    pairs.append((gain_to, units + 4 * groups, 1))
    stores = [
        pltpu.make_async_copy(full.at[pl.ds(place, count)], target, load_sem.at[index])
        for index, (target, place, count) in enumerate(pairs)
    ]
    for copy in stores:
        copy.start()
    for copy in stores:
        copy.wait()


def reduce_gradients(qkv, out, gain, mlp):
    dp_bits = bit_count(lax.axis_size("dp"))
    tensor = lax.axis_size("tensor")
    tensor_bits = bit_count(tensor)
    groups, units, width = out.shape[0] // tensor, mlp.shape[0], out.shape[-1]
    shared = 4 * groups + 1
    plan, total = stream_plan(units + shared, 2**dp_bits)
    bf16 = jnp.bfloat16
    dma = pltpu.SemaphoreType.DMA
    filler = total - units - shared

    def kernel(*refs):
        if filler:
            refs[8][pl.ds(units + shared, filler)] = jnp.zeros((filler, ROWS, width), bf16)
        reduce_kernel(plan, dp_bits, tensor_bits, groups, units, *refs)

    def buffer(count):
        return pltpu.VMEM((count, ROWS, width), bf16)

    return pl.pallas_call(
        kernel,
        out_shape=[
            jax.ShapeDtypeStruct((groups, ROWS, qkv.shape[-1]), bf16),
            jax.ShapeDtypeStruct((groups, ROWS, width), bf16),
            jax.ShapeDtypeStruct((1, ROWS, width), bf16),
            jax.ShapeDtypeStruct((units, ROWS, width), bf16),
        ],
        in_specs=[pl.BlockSpec(memory_space=pl.ANY)] * 4,
        out_specs=[pl.BlockSpec(memory_space=pl.ANY)] * 4,
        scratch_shapes=[
            buffer(total),
            buffer(shared * tensor),
            buffer(shared * (tensor - 1)),
            buffer(total),
            buffer(total),
            dma((len(plan), 2 * dp_bits)),
            dma((len(plan), 2 * dp_bits)),
            dma((tensor_bits,)),
            dma((tensor_bits,)),
            dma((max(6, 5 * tensor),)),
            dma((1,)),
        ],
        compiler_params=pltpu.CompilerParams(
            collective_id=0, has_side_effects=True, vmem_limit_bytes=40 * 2**20
        ),
        name="reduce_gradients",
    )(qkv, out, gain, mlp)


def body(layer_in, norm1_gain, qkv_weight, out_weight, norm2_gain, mlp_weight, cotangent):
    f32 = jnp.float32
    bf16 = jnp.bfloat16
    rows = layer_in.shape[0]
    width = layer_in.shape[1]
    span = SEQ // rows
    scale = HEAD_DIM ** (-0.5)
    first_norm_gain, second_norm_gain, w_qkv, w_out = (
        gather_rows(norm1_gain, "tensor"),
        gather_rows(norm2_gain, "tensor"),
        gather_rows(qkv_weight, "tensor"),
        gather_rows(out_weight, "tensor"),
    )
    first_norm_gain = first_norm_gain.astype(f32)
    second_norm_gain = second_norm_gain.astype(f32)
    position_slot = lax.axis_index("tensor") % span
    cosine, sine = rope_tables(position_slot * rows + jnp.arange(rows, dtype=jnp.int32))
    input_float_rows = layer_in.astype(f32)
    first_normed_rows, standardized_first, inverse_deviation_first = layer_norm_forward(
        input_float_rows, first_norm_gain
    )
    h1 = first_normed_rows.astype(bf16)
    qkv = jnp.dot(h1, w_qkv, preferred_element_type=f32)
    query = rotate(qkv[:, :width].reshape(rows, HEADS, HEAD_DIM), cosine, sine).astype(bf16)
    key_own = (
        rotate(qkv[:, width : 2 * width].reshape(rows, HEADS, HEAD_DIM), cosine, sine)
        .astype(bf16)
        .reshape(rows, width)
    )
    value_own = qkv[:, 2 * width :].astype(bf16)
    key_all, value_all = collect_keys(key_own, value_own, position_slot)
    keys = key_all.reshape(SEQ, HEADS, HEAD_DIM)
    values = value_all.reshape(SEQ, HEADS, HEAD_DIM)
    scores = jnp.einsum("qhd,khd->hqk", query, keys, preferred_element_type=f32) * scale
    total = jnp.log(jnp.sum(jnp.exp(scores), -1))
    probs_b = jnp.exp(scores - total[..., None]).astype(bf16)
    attended = (
        jnp.einsum("hqk,khd->qhd", probs_b, values, preferred_element_type=f32)
        .astype(bf16)
        .reshape(rows, width)
    )
    attention_mixed = input_float_rows + jnp.dot(attended, w_out, preferred_element_type=f32)
    second_normed_rows, standardized_second, inverse_deviation_second = layer_norm_forward(
        attention_mixed, second_norm_gain
    )
    h2 = second_normed_rows.astype(bf16)
    dz_f = cotangent.astype(f32)
    group = lax.all_gather(h2, "tensor", axis=0, tiled=True)
    gate_pre = jnp.dot(group, mlp_weight[0], preferred_element_type=f32)
    up_pre = jnp.dot(group, mlp_weight[1], preferred_element_type=f32)
    gel, slope = gelu_parts(gate_pre)
    hidden = (gel * up_pre).astype(bf16)
    branch = scatter_sum(right_product(hidden, mlp_weight[2]), "tensor", bf16)
    layer_out = (attention_mixed + branch).astype(bf16)
    grad_group = lax.all_gather(cotangent, "tensor", axis=0, tiled=True)
    grad_hidden = jnp.dot(grad_group, mlp_weight[2], preferred_element_type=f32)
    grad_gate = (grad_hidden * up_pre * slope).astype(bf16)
    grad_up = (grad_hidden * gel).astype(bf16)
    mlp_share = jnp.concatenate(
        [
            left_product(grad_gate, group).astype(bf16),
            left_product(grad_up, group).astype(bf16),
            left_product(hidden, grad_group).astype(bf16),
        ],
        0,
    )
    gradient_hidden_second = scatter_sum(
        right_product(grad_gate, mlp_weight[0]) + right_product(grad_up, mlp_weight[1]),
        "tensor",
        bf16,
    )
    second_norm_backward, gradient_gain_second = layer_norm_backward(
        gradient_hidden_second, standardized_second, inverse_deviation_second, second_norm_gain
    )
    grad_mixed = dz_f + second_norm_backward
    grad_mixed_b = grad_mixed.astype(bf16)
    grad_wout = left_product(attended, grad_mixed_b)
    grad_att = right_product(grad_mixed_b, w_out).astype(bf16).reshape(rows, HEADS, HEAD_DIM)
    scores = jnp.einsum("qhd,khd->hqk", query, keys, preferred_element_type=f32) * scale
    probs = jnp.exp(scores - total[..., None])
    probs_b = probs.astype(bf16)
    grad_probs = jnp.einsum("qhd,khd->hqk", grad_att, values, preferred_element_type=f32)
    delta = jnp.einsum(
        "qhd,qhd->hq", grad_att.astype(f32), attended.reshape(rows, HEADS, HEAD_DIM).astype(f32)
    )
    grad_scores = (probs * (grad_probs - delta[..., None])).astype(bf16)
    grad_query = jnp.einsum("hqk,khd->qhd", grad_scores, keys, preferred_element_type=f32) * scale
    grad_keys = jnp.einsum("hqk,qhd->khd", grad_scores, query, preferred_element_type=f32) * scale
    grad_values = jnp.einsum("hqk,qhd->khd", probs_b, grad_att, preferred_element_type=f32)
    key_total, value_total = return_grads(
        grad_keys.reshape(SEQ, width), grad_values.reshape(SEQ, width), position_slot
    )
    grad_q = unrotate(grad_query, cosine, sine).reshape(rows, width)
    grad_k = unrotate(key_total.reshape(rows, HEADS, HEAD_DIM), cosine, sine).reshape(rows, width)
    grad_qkv = jnp.concatenate([grad_q, grad_k, value_total], 1).astype(bf16)
    grad_wqkv = left_product(h1, grad_qkv)
    gradient_hidden_first = right_product(grad_qkv, w_qkv)
    first_norm_backward, gradient_gain_first = layer_norm_backward(
        gradient_hidden_first, standardized_first, inverse_deviation_first, first_norm_gain
    )
    input_grad = grad_mixed + first_norm_backward
    tensor = lax.axis_size("tensor")
    own = width // tensor
    units = mlp_weight.shape[2]
    gains = jnp.stack([gradient_gain_first, gradient_gain_second]).astype(bf16)
    gains = gains.reshape(2, tensor, own).transpose(1, 0, 2)
    gains = jnp.pad(gains, ((0, 0), (0, ROWS - 2), (0, width - own)))
    qkv_total, out_total, gain_total, mlp_total = reduce_gradients(
        to_groups(grad_wqkv.astype(bf16)), to_groups(grad_wout.astype(bf16)), gains,
        to_groups(mlp_share),
    )
    return (
        layer_out,
        input_grad,
        gain_total[0, 0, :own].astype(f32),
        qkv_total.reshape(own, 3 * width).astype(f32),
        out_total.reshape(own, width).astype(f32),
        gain_total[0, 1, :own].astype(f32),
        mlp_total.reshape(3, units, width).astype(f32).transpose(0, 2, 1),
    )


def solution(mesh):
    return jax.shard_map(
        body,
        mesh=mesh,
        in_specs=(
            P(("dp", "tensor"), None),
            P("tensor"),
            P("tensor", None),
            P("tensor", None),
            P("tensor"),
            P(None, None, "tensor"),
            P(("dp", "tensor"), None),
        ),
        out_specs=(
            P(("dp", "tensor"), None),
            P(("dp", "tensor"), None),
            P("tensor"),
            P("tensor", None),
            P("tensor", None),
            P("tensor"),
            P(None, None, "tensor"),
        ),
        check_vma=False,
    )
```

```python
import jax
import jax.numpy as jnp
from jax import lax
from jax.experimental import pallas as pl
from jax.experimental.pallas import tpu as pltpu
from jax.sharding import PartitionSpec as P

HEADS = 12
HEAD_DIM = 64
SEQ = 512


EPS = 1e-05
THETA = 160000.0


def swapped(value, axis, distance):
    mask = 2**distance
    pairs = [(source, source ^ mask) for source in range(lax.axis_size(axis))]
    return lax.ppermute(value, axis, pairs)


def rope_tables(positions):
    half = HEAD_DIM // 2
    freq = THETA ** (-jnp.arange(half).astype(jnp.float32) * 2.0 / HEAD_DIM)
    angle = positions.astype(jnp.float32)[:, None] * freq[None, :]
    return (jnp.cos(angle)[:, None, :], jnp.sin(angle)[:, None, :])


def rotate(values, cosine, sine):
    half = HEAD_DIM // 2
    first, second = (values[..., :half], values[..., half:])
    return jnp.concatenate([first * cosine - second * sine, second * cosine + first * sine], -1)


def unrotate(values, cosine, sine):
    half = HEAD_DIM // 2
    first, second = (values[..., :half], values[..., half:])
    return jnp.concatenate([first * cosine + second * sine, second * cosine - first * sine], -1)


def layer_norm_forward(values, gain):
    centred = values - jnp.mean(values, -1, keepdims=True)
    inverse = lax.rsqrt(jnp.mean(centred * centred, -1, keepdims=True) + EPS)
    normed = centred * inverse
    return (normed * gain, normed, inverse)


def layer_norm_backward(upstream, normed, inverse, gain):
    scaled = upstream * gain
    back = inverse * (
        scaled
        - jnp.mean(scaled, -1, keepdims=True)
        - normed * jnp.mean(scaled * normed, -1, keepdims=True)
    )
    return (back, jnp.sum(upstream * normed, 0))


def gelu_parts(values):
    cdf = 0.5 * (1.0 + jax.scipy.special.erf(values * 0.7071067811865476))
    density = jnp.exp(-0.5 * values * values) * 0.3989422804014327
    return (values * cdf, cdf + values * density)


def right_product(left, weight):
    return lax.dot_general(
        left, weight, (((1,), (1,)), ((), ())), preferred_element_type=jnp.float32
    )


def left_product(left, right):
    return lax.dot_general(
        left, right, (((0,), (0,)), ((), ())), preferred_element_type=jnp.float32
    )


def collect_keys(key_own, value_own, position_slot):
    pair = (key_own, value_own)
    far_key, far_value = swapped((pair[0], pair[1]), "tensor", 0)
    upper = (position_slot >> 0) % 2 == 1
    pair = (
        jnp.where(
            upper, jnp.concatenate([far_key, pair[0]], 0), jnp.concatenate([pair[0], far_key], 0)
        ),
        jnp.where(
            upper,
            jnp.concatenate([far_value, pair[1]], 0),
            jnp.concatenate([pair[1], far_value], 0),
        ),
    )
    return pair


def return_grads(key_grad, value_grad, position_slot):
    pair = (key_grad, value_grad)
    middle = pair[0].shape[0] // 2
    upper = (position_slot >> 0) % 2 == 1
    keep_key = jnp.where(upper, pair[0][middle:], pair[0][:middle])
    send_key = jnp.where(upper, pair[0][:middle], pair[0][middle:])
    keep_value = jnp.where(upper, pair[1][middle:], pair[1][:middle])
    send_value = jnp.where(upper, pair[1][:middle], pair[1][middle:])
    back_key = swapped(send_key.astype(jnp.bfloat16), "tensor", 0).astype(send_key.dtype)
    back_value = swapped(send_value.astype(jnp.bfloat16), "tensor", 0).astype(send_value.dtype)
    pair = (keep_key + back_key, keep_value + back_value)
    return pair


def bit_count(size):
    return size.bit_length() - 1


def gather_rows(value, axis):
    index = lax.axis_index(axis)
    for distance in range(bit_count(lax.axis_size(axis))):
        other = swapped(value, axis, distance)
        upper = (index >> distance) % 2 == 1
        value = jnp.where(
            upper, jnp.concatenate([other, value], 0), jnp.concatenate([value, other], 0)
        )
    return value


def scatter_sum(value, axis, wire):
    index = lax.axis_index(axis)
    for distance in reversed(range(bit_count(lax.axis_size(axis)))):
        middle = value.shape[0] // 2
        upper = (index >> distance) % 2 == 1
        keep = jnp.where(upper, value[middle:], value[:middle])
        send = jnp.where(upper, value[:middle], value[middle:])
        value = keep + swapped(send.astype(wire), axis, distance).astype(value.dtype)
    return value


ROWS = 8
MESH = pl.DeviceIdType.MESH


def to_groups(value):
    return value.reshape(-1, ROWS, value.shape[-1])


def add_into(result, result_start, target, start, source, source_start, count):
    step = 4
    while count % step:
        step //= 2

    def one(index, carry):
        shift = index * step
        result[pl.ds(result_start + shift, step)] = (
            target[pl.ds(start + shift, step)] + source[pl.ds(source_start + shift, step)]
        )
        return carry

    lax.fori_loop(0, count // step, one, 0)


def bit_of(index, bit):
    return lax.rem(lax.div(index, 2**bit), 2)


def partner_of(index, bit):
    return index + (1 - 2 * bit_of(index, bit)) * 2**bit


def link_orders(bits):
    if bits < 3:
        return [tuple(range(bits))] * 3
    rest = tuple(range(2, bits))
    return [(0, 1) + rest, rest + (0, 1), (1, 0) + rest]


def halvings(count, bits):
    stages = 0
    while stages < bits and (count >> stages) % 2 == 0:
        stages += 1
    return stages


def sum_stage(values, stage):
    index = lax.axis_index("dp")
    bits = bit_count(lax.axis_size("dp"))
    if stage >= bits:
        return values
    results = []
    for value, order in zip(values, link_orders(bits)):
        bit = order[stage]
        if value.shape[0] % 2 == 0:
            middle = value.shape[0] // 2
            upper = (index >> bit) % 2 == 1
            keep = jnp.where(upper, value[middle:], value[:middle])
            send = jnp.where(upper, value[:middle], value[middle:])
        else:
            keep = send = value
        results.append(keep + swapped(send, "dp", bit))
    return results


def tied(value, chunks):
    value, *chunks = lax.optimization_barrier((value, *chunks))
    return value, chunks


def stream_plan(total, devices):
    units = -(-total // devices)
    orders = link_orders(bit_count(devices))
    weights = [5, 3, 5]
    orders, weights = orders * 2, weights * 2
    shares = [units * weight // sum(weights) for weight in weights]
    for index in range(units - sum(shares)):
        shares[index % len(shares)] += 1
    plan, begin = [], 0
    for order, share in zip(orders, shares):
        if share:
            plan.append((order, begin, share * devices))
            begin += share * devices
    return plan, begin


def reduce_kernel(
    plan, dp_bits, tensor_bits, groups, units, qkv_ref, out_ref, gain_ref, mlp_ref,
    qkv_to, out_to, gain_to, mlp_to, acc, work, got_tensor, got, full, whole,
    send_sem, recv_sem, tensor_send, tensor_recv, load_sem, mlp_sem, piece_send, piece_recv,
):
    me = lax.axis_index("dp")
    slot = lax.axis_index("tensor")
    tensor = 2**tensor_bits
    width = acc.shape[-1]
    shared = 4 * groups + 1

    piece = units // 3
    stages = halvings(piece, dp_bits)
    chunk = piece >> stages
    places, piece_loads = [], []
    for index, order in enumerate(link_orders(dp_bits)):
        places.append([index * piece])
        for stage in range(stages):
            step = bit_of(me, order[stage]) * (piece >> (stage + 1))
            places[index].append(places[index][stage] + step)
        copy = pltpu.make_async_copy(
            mlp_ref.at[pl.ds(index * chunk, chunk)],
            whole.at[pl.ds(places[index][stages], chunk)],
            mlp_sem.at[index],
        )
        copy.start()
        piece_loads.append(copy)

    def piece_copy(index, stage):
        region = pl.ds(places[index][stage + 1], piece >> (stage + 1))
        return pltpu.make_async_remote_copy(
            src_ref=whole.at[region],
            dst_ref=whole.at[region],
            send_sem=piece_send.at[index, stage],
            recv_sem=piece_recv.at[index, stage],
            device_id=(partner_of(me, link_orders(dp_bits)[index][stage]), slot),
            device_id_type=MESH,
        )

    loads = []
    for part in range(tensor):
        rows = pl.ds(part * groups, groups)
        pairs = [
            (qkv_ref.at[rows, :, pl.ds(block * width, width)], block * groups, groups)
            for block in range(3)
        ]
        pairs.append((out_ref.at[rows], 3 * groups, groups))
        pairs.append((gain_ref.at[pl.ds(part, 1)], 4 * groups, 1))
        for source, place, count in pairs:
            copy = pltpu.make_async_copy(
                source, work.at[pl.ds(part * shared + place, count)], load_sem.at[len(loads)]
            )
            copy.start()
            loads.append(copy)

    barrier = pltpu.get_barrier_semaphore()
    for bit in range(dp_bits):
        pl.semaphore_signal(
            barrier, inc=1, device_id=(partner_of(me, bit), slot), device_id_type=MESH
        )
    for bit in range(tensor_bits):
        pl.semaphore_signal(
            barrier, inc=1, device_id=(me, partner_of(slot, bit)), device_id_type=MESH
        )
    for copy in piece_loads:
        copy.wait()
    pl.semaphore_wait(barrier, dp_bits + tensor_bits)

    starts = [[begin] for _, begin, _ in plan]

    def reduce_copy(stream, stage):
        order, base, share = plan[stream]
        bit = order[stage]
        half = share >> (stage + 1)
        begin = starts[stream][stage]
        return pltpu.make_async_remote_copy(
            src_ref=acc.at[pl.ds(begin + (1 - bit_of(me, bit)) * half, half)],
            dst_ref=got.at[pl.ds(base + share - (share >> stage), half)],
            send_sem=send_sem.at[stream, stage],
            recv_sem=recv_sem.at[stream, stage],
            device_id=(partner_of(me, bit), slot),
            device_id_type=MESH,
        )

    def gather_copy(stream, stage):
        order, _, share = plan[stream]
        region = pl.ds(starts[stream][stage + 1], share >> (stage + 1))
        return pltpu.make_async_remote_copy(
            src_ref=full.at[region],
            dst_ref=full.at[region],
            send_sem=send_sem.at[stream, dp_bits + stage],
            recv_sem=recv_sem.at[stream, dp_bits + stage],
            device_id=(partner_of(me, order[stage]), slot),
            device_id_type=MESH,
        )

    moving = []
    if stages:
        moving = [piece_copy(index, stages - 1) for index in range(3)]
        for copy in moving:
            copy.start()

    for copy in loads:
        copy.wait()
    start, length, place = 0, shared * tensor, 0
    for stage, bit in enumerate(reversed(range(tensor_bits))):
        length //= 2
        mine = bit_of(slot, bit)
        copy = pltpu.make_async_remote_copy(
            src_ref=work.at[pl.ds(start + (1 - mine) * length, length)],
            dst_ref=got_tensor.at[pl.ds(place, length)],
            send_sem=tensor_send.at[stage],
            recv_sem=tensor_recv.at[stage],
            device_id=(me, partner_of(slot, bit)),
            device_id_type=MESH,
        )
        copy.start()
        copy.wait()
        start = start + mine * length
        if stage + 1 < tensor_bits:
            add_into(work, start, work, start, got_tensor, place, length)
        else:
            add_into(acc, 0, work, start, got_tensor, place, length)
        place += length
    flying = []
    for stream in range(len(plan)):
        flying.append(reduce_copy(stream, 0))
        flying[stream].start()

    for stage in range(dp_bits):
        for stream, (order, base, share) in enumerate(plan):
            flying[stream].wait()
            half = share >> (stage + 1)
            begin = starts[stream][stage] + bit_of(me, order[stage]) * half
            starts[stream].append(begin)
            last = stage + 1 == dp_bits
            add_into(
                full if last else acc, begin, acc, begin,
                got, base + share - (share >> stage), half,
            )
            copy = gather_copy(stream, stage) if last else reduce_copy(stream, stage + 1)
            copy.start()
            flying[stream] = copy
        ahead = stages - 1 - stage
        if ahead >= 0:
            for index in range(3):
                moving[index].wait()
                if ahead:
                    moving[index] = piece_copy(index, ahead - 1)
                    moving[index].start()
    store_mlp = pltpu.make_async_copy(whole, mlp_to, mlp_sem.at[0])
    store_mlp.start()
    for stage in reversed(range(dp_bits)):
        for stream in range(len(plan)):
            flying[stream].wait()
            if stage:
                copy = gather_copy(stream, stage - 1)
                copy.start()
                flying[stream] = copy
    pairs = []
    for block in range(3):
        target = qkv_to.at[:, :, pl.ds(block * width, width)]
        pairs.append((target, block * groups, groups))
    pairs.append((out_to, 3 * groups, groups))
    pairs.append((gain_to, 4 * groups, 1))
    stores = [
        pltpu.make_async_copy(full.at[pl.ds(place, count)], target, load_sem.at[index])
        for index, (target, place, count) in enumerate(pairs)
    ]
    for copy in stores:
        copy.start()
    for copy in stores:
        copy.wait()
    store_mlp.wait()


def reduce_gradients(qkv, out, gain, mlp, units):
    dp_bits = bit_count(lax.axis_size("dp"))
    tensor = lax.axis_size("tensor")
    tensor_bits = bit_count(tensor)
    groups, width = out.shape[0] // tensor, out.shape[-1]
    stages = max(1, halvings(units // 3, dp_bits))
    shared = 4 * groups + 1
    plan, total = stream_plan(shared, 2**dp_bits)
    bf16 = jnp.bfloat16
    dma = pltpu.SemaphoreType.DMA
    filler = total - shared

    def kernel(*refs):
        if filler:
            refs[8][pl.ds(shared, filler)] = jnp.zeros((filler, ROWS, width), bf16)
        reduce_kernel(plan, dp_bits, tensor_bits, groups, units, *refs)

    def buffer(count):
        return pltpu.VMEM((count, ROWS, width), bf16)

    return pl.pallas_call(
        kernel,
        out_shape=[
            jax.ShapeDtypeStruct((groups, ROWS, qkv.shape[-1]), bf16),
            jax.ShapeDtypeStruct((groups, ROWS, width), bf16),
            jax.ShapeDtypeStruct((1, ROWS, width), bf16),
            jax.ShapeDtypeStruct((units, ROWS, width), bf16),
        ],
        in_specs=[pl.BlockSpec(memory_space=pl.ANY)] * 4,
        out_specs=[pl.BlockSpec(memory_space=pl.ANY)] * 4,
        scratch_shapes=[
            buffer(total),
            buffer(shared * tensor),
            buffer(shared * (tensor - 1)),
            buffer(total),
            buffer(total),
            buffer(units),
            dma((len(plan), 2 * dp_bits)),
            dma((len(plan), 2 * dp_bits)),
            dma((tensor_bits,)),
            dma((tensor_bits,)),
            dma((max(6, 5 * tensor),)),
            dma((3,)),
            dma((3, stages)),
            dma((3, stages)),
        ],
        compiler_params=pltpu.CompilerParams(
            collective_id=0, has_side_effects=True, vmem_limit_bytes=40 * 2**20
        ),
        name="reduce_gradients",
    )(qkv, out, gain, mlp)


def body(layer_in, norm1_gain, qkv_weight, out_weight, norm2_gain, mlp_weight, cotangent):
    f32 = jnp.float32
    bf16 = jnp.bfloat16
    rows = layer_in.shape[0]
    width = layer_in.shape[1]
    span = SEQ // rows
    scale = HEAD_DIM ** (-0.5)
    first_norm_gain, second_norm_gain, w_qkv, w_out = (
        gather_rows(norm1_gain, "tensor"),
        gather_rows(norm2_gain, "tensor"),
        gather_rows(qkv_weight, "tensor"),
        gather_rows(out_weight, "tensor"),
    )
    first_norm_gain = first_norm_gain.astype(f32)
    second_norm_gain = second_norm_gain.astype(f32)
    position_slot = lax.axis_index("tensor") % span
    cosine, sine = rope_tables(position_slot * rows + jnp.arange(rows, dtype=jnp.int32))
    input_float_rows = layer_in.astype(f32)
    first_normed_rows, standardized_first, inverse_deviation_first = layer_norm_forward(
        input_float_rows, first_norm_gain
    )
    h1 = first_normed_rows.astype(bf16)
    qkv = jnp.dot(h1, w_qkv, preferred_element_type=f32)
    query = rotate(qkv[:, :width].reshape(rows, HEADS, HEAD_DIM), cosine, sine).astype(bf16)
    key_own = (
        rotate(qkv[:, width : 2 * width].reshape(rows, HEADS, HEAD_DIM), cosine, sine)
        .astype(bf16)
        .reshape(rows, width)
    )
    value_own = qkv[:, 2 * width :].astype(bf16)
    key_all, value_all = collect_keys(key_own, value_own, position_slot)
    keys = key_all.reshape(SEQ, HEADS, HEAD_DIM)
    values = value_all.reshape(SEQ, HEADS, HEAD_DIM)
    scores = jnp.einsum("qhd,khd->hqk", query, keys, preferred_element_type=f32) * scale
    highest = jnp.max(scores, -1)
    total = highest + jnp.log(jnp.sum(jnp.exp(scores - highest[..., None]), -1))
    total = lax.optimization_barrier(total)
    probs_b = jnp.exp(scores - total[..., None]).astype(bf16)
    attended = (
        jnp.einsum("hqk,khd->qhd", probs_b, values, preferred_element_type=f32)
        .astype(bf16)
        .reshape(rows, width)
    )
    attention_mixed = input_float_rows + jnp.dot(attended, w_out, preferred_element_type=f32)
    second_normed_rows, standardized_second, inverse_deviation_second = layer_norm_forward(
        attention_mixed, second_norm_gain
    )
    h2 = second_normed_rows.astype(bf16)
    dz_f = cotangent.astype(f32)
    group = lax.all_gather(h2, "tensor", axis=0, tiled=True)
    gate_pre = jnp.dot(group, mlp_weight[0], preferred_element_type=f32)
    up_pre = jnp.dot(group, mlp_weight[1], preferred_element_type=f32)
    gel, slope = gelu_parts(gate_pre)
    hidden = (gel * up_pre).astype(bf16)
    branch = scatter_sum(right_product(hidden, mlp_weight[2]), "tensor", bf16)
    layer_out = (attention_mixed + branch).astype(bf16)
    grad_group = lax.all_gather(cotangent, "tensor", axis=0, tiled=True)
    grad_hidden = jnp.dot(grad_group, mlp_weight[2], preferred_element_type=f32)
    grad_gate = (grad_hidden * up_pre * slope).astype(bf16)
    grad_up = (grad_hidden * gel).astype(bf16)
    mlp_pieces = [
        to_groups(left_product(left, right).astype(bf16))
        for left, right in ((grad_gate, group), (grad_up, group), (hidden, grad_group))
    ]
    mlp_chunks = sum_stage(mlp_pieces, 0)
    gradient_hidden_second = scatter_sum(
        right_product(grad_gate, mlp_weight[0]) + right_product(grad_up, mlp_weight[1]),
        "tensor",
        bf16,
    )
    second_norm_backward, gradient_gain_second = layer_norm_backward(
        gradient_hidden_second, standardized_second, inverse_deviation_second, second_norm_gain
    )
    grad_mixed = dz_f + second_norm_backward
    grad_mixed_b = grad_mixed.astype(bf16)
    grad_wout = left_product(attended, grad_mixed_b)
    grad_att, mlp_chunks = tied(right_product(grad_mixed_b, w_out).astype(bf16), mlp_chunks)
    grad_att = grad_att.reshape(rows, HEADS, HEAD_DIM)
    mlp_chunks = sum_stage(mlp_chunks, 1)
    scores = jnp.einsum("qhd,khd->hqk", query, keys, preferred_element_type=f32) * scale
    probs = jnp.exp(scores - total[..., None])
    probs_b = probs.astype(bf16)
    grad_probs = jnp.einsum("qhd,khd->hqk", grad_att, values, preferred_element_type=f32)
    delta = jnp.einsum(
        "qhd,qhd->hq", grad_att.astype(f32), attended.reshape(rows, HEADS, HEAD_DIM).astype(f32)
    )
    grad_scores = (probs * (grad_probs - delta[..., None])).astype(bf16)
    grad_scores, mlp_chunks = tied(grad_scores, mlp_chunks)
    mlp_chunks = sum_stage(mlp_chunks, 2)
    grad_query = jnp.einsum("hqk,khd->qhd", grad_scores, keys, preferred_element_type=f32) * scale
    grad_keys = jnp.einsum("hqk,qhd->khd", grad_scores, query, preferred_element_type=f32) * scale
    grad_values = jnp.einsum("hqk,qhd->khd", probs_b, grad_att, preferred_element_type=f32)
    key_total, value_total = return_grads(
        grad_keys.reshape(SEQ, width), grad_values.reshape(SEQ, width), position_slot
    )
    grad_q = unrotate(grad_query, cosine, sine).reshape(rows, width)
    grad_k = unrotate(key_total.reshape(rows, HEADS, HEAD_DIM), cosine, sine).reshape(rows, width)
    grad_qkv = jnp.concatenate([grad_q, grad_k, value_total], 1).astype(bf16)
    grad_wqkv = left_product(h1, grad_qkv)
    grad_qkv, mlp_chunks = tied(grad_qkv, mlp_chunks)
    for stage in range(3, bit_count(lax.axis_size("dp"))):
        mlp_chunks = sum_stage(mlp_chunks, stage)
    gradient_hidden_first = right_product(grad_qkv, w_qkv)
    first_norm_backward, gradient_gain_first = layer_norm_backward(
        gradient_hidden_first, standardized_first, inverse_deviation_first, first_norm_gain
    )
    input_grad = grad_mixed + first_norm_backward
    tensor = lax.axis_size("tensor")
    own = width // tensor
    units = mlp_weight.shape[2]
    gains = jnp.stack([gradient_gain_first, gradient_gain_second]).astype(bf16)
    gains = gains.reshape(2, tensor, own).transpose(1, 0, 2)
    gains = jnp.pad(gains, ((0, 0), (0, ROWS - 2), (0, width - own)))
    qkv_total, out_total, gain_total, mlp_total = reduce_gradients(
        to_groups(grad_wqkv.astype(bf16)), to_groups(grad_wout.astype(bf16)), gains,
        jnp.concatenate(mlp_chunks, 0), 3 * mlp_pieces[0].shape[0],
    )
    return (
        layer_out,
        input_grad,
        gain_total[0, 0, :own].astype(f32),
        qkv_total.reshape(own, 3 * width).astype(f32),
        out_total.reshape(own, width).astype(f32),
        gain_total[0, 1, :own].astype(f32),
        mlp_total.reshape(3, units, width).astype(f32).transpose(0, 2, 1),
    )


def solution(mesh):
    return jax.shard_map(
        body,
        mesh=mesh,
        in_specs=(
            P(("dp", "tensor"), None),
            P("tensor"),
            P("tensor", None),
            P("tensor", None),
            P("tensor"),
            P(None, None, "tensor"),
            P(("dp", "tensor"), None),
        ),
        out_specs=(
            P(("dp", "tensor"), None),
            P(("dp", "tensor"), None),
            P("tensor"),
            P("tensor", None),
            P("tensor", None),
            P("tensor"),
            P(None, None, "tensor"),
        ),
        check_vma=False,
    )
```
